32 devices in a mesh: fsdp: 8 (over y, x, core), tp: 4 (over z).
Axes of the slice: x: 2, y: 2, z: 4, core: 2. Of those that a mesh axis runs over, the one named last changes fastest.
Arguments:
- layer_input: bfloat16 [4096, 768], P(('fsdp', 'tp')), may hold values from -13 to 13
- seq_lengths: int32 [8], P('fsdp'), may hold values from 8 to 512
- query_weight: bfloat16 [768, 768], P('fsdp', 'tp')
- query_bias: float32 [768], P('tp'), may hold values from -3 to 3
- key_weight: bfloat16 [768, 768], P('fsdp', 'tp')
- value_weight: bfloat16 [768, 768], P('fsdp', 'tp'), may hold values from -0.21875 to 0.21875
- value_bias: float32 [768], P('tp'), may hold values from -3 to 3
- output_weight: bfloat16 [768, 768], P('tp', 'fsdp'), may hold values from -1.75 to 1.75
- output_bias: float32 [768], replicated, may hold values from -3 to 3
- first_gain: float32 [768], replicated, may hold values from 0.5 to 1.5
- first_shift: float32 [768], replicated, may hold values from -3 to 3
- inner_weight: bfloat16 [768, 3072], P('fsdp', 'tp'), may hold values from -0.21875 to 0.21875
- inner_bias: float32 [3072], P('tp'), may hold values from -3 to 3
- outer_weight: bfloat16 [3072, 768], P('tp', 'fsdp'), may hold values from -0.109375 to 0.109375
- outer_bias: float32 [768], replicated, may hold values from -3 to 3
- second_gain: float32 [768], replicated, may hold values from 0.5 to 1.5
- second_shift: float32 [768], replicated, may hold values from -3 to 3
- cotangent: bfloat16 [4096, 768], P(('fsdp', 'tp')), may hold values from -26 to 26
Outputs:
- layer_output: bfloat16 [4096, 768], P(('fsdp', 'tp'))
- input_grad: float32 [4096, 768], P(('fsdp', 'tp'))
- query_weight_grad: float32 [768, 768], P('fsdp', 'tp')
- query_bias_grad: float32 [768], replicated
- key_weight_grad: float32 [768, 768], P('fsdp', 'tp')
- value_weight_grad: float32 [768, 768], P('fsdp', 'tp')
- value_bias_grad: float32 [768], replicated
- output_weight_grad: float32 [768, 768], P('tp', 'fsdp')
- output_bias_grad: float32 [768], replicated
- first_gain_grad: float32 [768], replicated
- first_shift_grad: float32 [768], replicated
- inner_weight_grad: float32 [768, 3072], P('fsdp', 'tp')
- inner_bias_grad: float32 [3072], replicated
- outer_weight_grad: float32 [3072, 768], P('tp', 'fsdp')
- outer_bias_grad: float32 [768], replicated
- second_gain_grad: float32 [768], replicated
- second_shift_grad: float32 [768], replicated
The draws below stay inside these ranges and needn't reach their ends.
Inputs may be any that keep to these rules, and one draw needn't show every extreme that they name: `seq_lengths`: positions at or beyond a sequence's length are padding; no sequence is empty.
All inputs are finite; a program needn't handle non-finite values.
Results may differ from the reference program's by a relative error of at most 0.014.
The reference program's roundings to bfloat16 on the way (of `queries`, `probs`, `context`, `active`, `grad_context` and `grad_scores`) count: a program that leaves them out, or rounds other values in their place, can miss the bound.
Values may be sent and summed in bfloat16 or wider, within the bound.
No kernel may reach another device: no remote copies, remote signals or barrier semaphores. Data moves between devices by JAX's collectives and lax.ppermute only.
A program may use at most 64 MiB of HBM per device.

```python
import jax
import jax.numpy as jnp
from jax import lax

D = 768
HEADS = 12
FF = 3072
HEAD_DIM = 64
SEQ_LEN = 512
SEQS = 8
TOKENS = 4096


def draw_layer_input(key, part):
    base = jnp.clip(jax.random.normal(jax.random.fold_in(key, 1), (TOKENS, D), jnp.float32), -6.0, 6.0)
    return base.astype(jnp.bfloat16)


def query_key_pair(key):
    first = jnp.clip(jax.random.normal(jax.random.fold_in(key, 21), (D, D), jnp.float32), -6.0, 6.0) * D ** (-0.5)
    second = jnp.clip(jax.random.normal(jax.random.fold_in(key, 22), (D, D), jnp.float32), -6.0, 6.0) * D ** (-0.5)
    return (first, second)


def draw_query_weight(key, part):
    return query_key_pair(key)[0].astype(jnp.bfloat16)


def draw_key_weight(key, part):
    return query_key_pair(key)[1].astype(jnp.bfloat16)


def draw_cotangent(key, part):
    base = jnp.clip(jax.random.normal(jax.random.fold_in(key, 31), (TOKENS, D), jnp.float32), -6.0, 6.0)
    rising = 1.0 + 2.0 * jnp.arange(TOKENS, dtype=jnp.float32)[:, None] / (TOKENS - 1)
    return (base * rising).astype(jnp.bfloat16)


def touch_ends(entries, stream_key, low, largest):
    index_at = [jax.random.randint(jax.random.fold_in(stream_key, axis), (), 0, length) for axis, length in enumerate(entries.shape)]
    main_axis = entries.shape.index(max(entries.shape))
    beside = index_at[:main_axis] + [(index_at[main_axis] + 1) % entries.shape[main_axis]] + index_at[main_axis + 1:]
    return entries.at[tuple(index_at)].set(low).at[tuple(beside)].set(largest)


def levels(stream_key, shape, cuts, least, largest):
    def one(position, parts):
        steps = jax.random.uniform(jax.random.fold_in(jax.random.fold_in(stream_key, 6), position), (parts,), jnp.float32, least / len(cuts), largest / len(cuts))
        return jnp.repeat(jnp.exp(steps), shape[position] // parts).reshape((-1,) + (1,) * (len(shape) - position - 1))

    level = one(*cuts[0])
    for cut in cuts[1:]:
        level = level * one(*cut)
    return level


def noise(own_key, dims, deviation, bound, split=(), held_as=jnp.bfloat16):
    values = jax.random.normal(own_key, dims, jnp.float32) * deviation
    if len(split) > 0:
        values = levels(own_key, dims, split, -0.22, 0.18) * values
    return jnp.clip(values, min=-bound, max=bound).astype(held_as)


def setup_inputs(seed: int = 0) -> dict:
    key_list = jax.random.split(jax.random.key(seed), 19)
    return {
        "layer_input": draw_layer_input(jax.random.fold_in(key_list[18], 71), 0),
        "seq_lengths": touch_ends(jax.random.randint(key_list[1], (SEQS,), 8, SEQ_LEN + 1), jax.random.fold_in(key_list[1], 1), 8, SEQ_LEN).astype(jnp.int32),
        "query_weight": draw_query_weight(jax.random.fold_in(key_list[18], 71), 0),
        "query_bias": noise(key_list[3], (D,), 0.5, 3.0, ((0, 4),), jnp.float32),
        "key_weight": draw_key_weight(jax.random.fold_in(key_list[18], 71), 0),
        "value_weight": noise(key_list[5], (D, D), D ** -0.5, 0.21875, ((0, 8), (1, 4))),
        "value_bias": noise(key_list[6], (D,), 0.5, 3.0, ((0, 4),), jnp.float32),
        "output_weight": noise(key_list[7], (D, D), (D // 64) ** -0.5, 1.75, ((0, 4), (1, 8))),
        "output_bias": noise(key_list[8], (D,), 0.5, 3.0, (), jnp.float32),
        "first_gain": jnp.clip(1.0 + 0.1 * jax.random.normal(key_list[9], (D,), jnp.float32), 0.5, 1.5),
        "first_shift": noise(key_list[10], (D,), 0.5, 3.0, (), jnp.float32),
        "inner_weight": noise(key_list[11], (D, FF), D ** -0.5, 0.21875, ((0, 8), (1, 4))),
        "inner_bias": noise(key_list[12], (FF,), 0.5, 3.0, ((0, 4),), jnp.float32),
        "outer_weight": noise(key_list[13], (FF, D), FF ** -0.5, 0.109375, ((0, 4), (1, 8))),
        "outer_bias": noise(key_list[14], (D,), 0.5, 3.0, (), jnp.float32),
        "second_gain": jnp.clip(1.0 + 0.1 * jax.random.normal(key_list[15], (D,), jnp.float32), 0.5, 1.5),
        "second_shift": noise(key_list[16], (D,), 0.5, 3.0, (), jnp.float32),
        "cotangent": draw_cotangent(jax.random.fold_in(key_list[18], 71), 0),
    }


epsilon = 1e-05

def matmul(left, right):
    return jnp.dot(left, right, preferred_element_type=jnp.float32)

def transposed(left, right):
    return lax.dot_general(left, right, (((0,), (0,)), ((), ())), preferred_element_type=jnp.float32)

def right_transposed(left, right):
    return lax.dot_general(left, right, (((1,), (1,)), ((), ())), preferred_element_type=jnp.float32)

def layer_norm(values, gain, shift):
    centre = values - lax.optimization_barrier(jnp.mean(values, axis=-1, keepdims=True))
    inverse = lax.rsqrt(lax.optimization_barrier(jnp.mean(centre * centre, axis=-1, keepdims=True)) + epsilon)
    normed = centre * inverse
    return (normed * gain + shift, normed, inverse)

def norm_backward(upstream, normed, inverse, gain):
    scaled = upstream * gain
    return inverse * (scaled - lax.optimization_barrier(jnp.mean(scaled, axis=-1, keepdims=True)) - normed * lax.optimization_barrier(jnp.mean(scaled * normed, axis=-1, keepdims=True)))

def gelu_value(pre):
    return pre * 0.5 * (1.0 + jax.scipy.special.erf(pre * 0.7071067811865476))

def gelu_slope(pre):
    return 0.5 * (1.0 + jax.scipy.special.erf(pre * 0.7071067811865476)) + pre * jnp.exp(-0.5 * pre * pre) * 0.3989422804014327

def head_view(matrix):
    return matrix.astype(jnp.float32).reshape(matrix.shape[0], HEADS, HEAD_DIM)

def masked_scores(queries, key_rows, length):
    scores = jnp.einsum('qhd,khd->hqk', head_view(queries), head_view(key_rows)) * HEAD_DIM ** (-0.5)
    valid = jnp.arange(SEQ_LEN, dtype=jnp.int32) < length
    return jnp.where(valid[None, None, :], scores, -jnp.inf)

def one_sequence(params, seq_input, seq_cot, length):
    query_weight, query_bias, key_weight, value_weight, value_bias, output_weight, output_bias, first_gain, first_shift, inner_weight, inner_bias, outer_weight, outer_bias, second_gain, second_shift = params
    queries = (matmul(seq_input, query_weight) + query_bias).astype(jnp.bfloat16)
    key_rows = matmul(seq_input, key_weight).astype(jnp.bfloat16)
    value_rows = (matmul(seq_input, value_weight) + value_bias).astype(jnp.bfloat16)
    scores = masked_scores(queries, key_rows, length)
    top = lax.optimization_barrier(jnp.max(scores, axis=-1, keepdims=True))
    lse = top + jnp.log(lax.optimization_barrier(jnp.sum(jnp.exp(scores - top), axis=-1, keepdims=True)))
    probs = jnp.exp(scores - lse).astype(jnp.bfloat16)
    context = jnp.einsum('hqk,khd->qhd', probs.astype(jnp.float32), head_view(value_rows))
    context = context.reshape(SEQ_LEN, D).astype(jnp.bfloat16)
    first_sum = seq_input.astype(jnp.float32) + matmul(context, output_weight) + output_bias
    hidden, first_normed, first_inverse = layer_norm(first_sum, first_gain, first_shift)
    hidden_half = hidden.astype(jnp.bfloat16)
    pre = matmul(hidden_half, inner_weight) + inner_bias
    active = gelu_value(pre).astype(jnp.bfloat16)
    second_sum = hidden + matmul(active, outer_weight) + outer_bias
    result, second_normed, second_inverse = layer_norm(second_sum, second_gain, second_shift)
    output = result.astype(jnp.bfloat16)
    upstream = seq_cot.astype(jnp.float32)
    second_gain_grad = lax.optimization_barrier(jnp.sum(upstream * second_normed, axis=0))
    second_shift_grad = lax.optimization_barrier(jnp.sum(upstream, axis=0))
    grad_second = norm_backward(upstream, second_normed, second_inverse, second_gain)
    grad_second_half = grad_second.astype(jnp.bfloat16)
    outer_weight_grad = transposed(active, grad_second_half)
    outer_bias_grad = lax.optimization_barrier(jnp.sum(grad_second, axis=0))
    grad_pre = right_transposed(grad_second_half, outer_weight) * gelu_slope(pre)
    inner_bias_grad = lax.optimization_barrier(jnp.sum(grad_pre, axis=0))
    grad_pre_half = grad_pre.astype(jnp.bfloat16)
    inner_weight_grad = transposed(hidden_half, grad_pre_half)
    grad_hidden = grad_second + right_transposed(grad_pre_half, inner_weight)
    first_gain_grad = lax.optimization_barrier(jnp.sum(grad_hidden * first_normed, axis=0))
    first_shift_grad = lax.optimization_barrier(jnp.sum(grad_hidden, axis=0))
    grad_first = norm_backward(grad_hidden, first_normed, first_inverse, first_gain)
    grad_first_half = grad_first.astype(jnp.bfloat16)
    output_weight_grad = transposed(context, grad_first_half)
    output_bias_grad = lax.optimization_barrier(jnp.sum(grad_first, axis=0))
    grad_context = right_transposed(grad_first_half, output_weight).astype(jnp.bfloat16)
    probs_full = jnp.exp(masked_scores(queries, key_rows, length) - lse)
    context_heads = head_view(grad_context)
    grad_value = jnp.einsum('hqk,qhd->khd', probs_full.astype(jnp.bfloat16).astype(jnp.float32), context_heads)
    grad_probs = jnp.einsum('qhd,khd->hqk', context_heads, head_view(value_rows))
    delta = lax.optimization_barrier(jnp.sum(probs_full * grad_probs, axis=-1, keepdims=True))
    grad_scores = (probs_full * (grad_probs - delta) * HEAD_DIM ** (-0.5)).astype(jnp.bfloat16).astype(jnp.float32)
    grad_query = jnp.einsum('hqk,khd->qhd', grad_scores, head_view(key_rows)).reshape(SEQ_LEN, D)
    grad_key = jnp.einsum('hqk,qhd->khd', grad_scores, head_view(queries)).reshape(SEQ_LEN, D)
    grad_value = grad_value.reshape(SEQ_LEN, D)
    query_bias_grad = lax.optimization_barrier(jnp.sum(grad_query, axis=0))
    value_bias_grad = lax.optimization_barrier(jnp.sum(grad_value, axis=0))
    query_half = grad_query.astype(jnp.bfloat16)
    key_half = grad_key.astype(jnp.bfloat16)
    value_half = grad_value.astype(jnp.bfloat16)
    query_weight_grad = transposed(seq_input, query_half)
    key_weight_grad = transposed(seq_input, key_half)
    value_weight_grad = transposed(seq_input, value_half)
    input_grad = grad_first + right_transposed(query_half, query_weight) + right_transposed(key_half, key_weight) + right_transposed(value_half, value_weight)
    grads = (query_weight_grad, query_bias_grad, key_weight_grad, value_weight_grad, value_bias_grad, output_weight_grad, output_bias_grad, first_gain_grad, first_shift_grad, inner_weight_grad, inner_bias_grad, outer_weight_grad, outer_bias_grad, second_gain_grad, second_shift_grad)
    return (output, input_grad, grads)

def reference(layer_input, seq_lengths, query_weight, query_bias, key_weight, value_weight, value_bias, output_weight, output_bias, first_gain, first_shift, inner_weight, inner_bias, outer_weight, outer_bias, second_gain, second_shift, cotangent):
    params = (query_weight, query_bias, key_weight, value_weight, value_bias, output_weight, output_bias, first_gain, first_shift, inner_weight, inner_bias, outer_weight, outer_bias, second_gain, second_shift)
    inputs = layer_input.reshape(-1, SEQ_LEN, D)
    cots = cotangent.reshape(-1, SEQ_LEN, D)
    initial = tuple((jnp.zeros(param.shape, jnp.float32) for param in params))

    def step(carry, item):
        seq_input, seq_cot, length = item
        output, input_grad, grads = one_sequence(params, seq_input, seq_cot, length)
        carry = tuple((total + grad for total, grad in zip(carry, grads)))
        return (carry, (output, input_grad))
    totals, (outputs, input_grads) = lax.scan(step, initial, (inputs, cots, seq_lengths))
    return (outputs.reshape(-1, D), input_grads.reshape(-1, D)) + totals
```

```python
import jax
import jax.numpy as jnp
from jax import lax
from jax.sharding import PartitionSpec as P

HEAD_DIM = 64
epsilon = 1e-05
half_type = jnp.bfloat16


def matmul(left, right):
    return jnp.dot(left, right, preferred_element_type=jnp.float32)


def transposed(left, right):
    return lax.dot_general(
        left, right, (((0,), (0,)), ((), ())), preferred_element_type=jnp.float32
    )


def right_transposed(left, right):
    return lax.dot_general(
        left, right, (((1,), (1,)), ((), ())), preferred_element_type=jnp.float32
    )


def layer_norm(values, gain, shift):
    centre = values - jnp.mean(values, axis=-1, keepdims=True)
    inverse = lax.rsqrt(jnp.mean(centre * centre, axis=-1, keepdims=True) + epsilon)
    normed = centre * inverse
    return (normed * gain + shift, normed, inverse)


def norm_backward(upstream, normed, inverse, gain):
    scaled = upstream * gain
    return inverse * (
        scaled
        - jnp.mean(scaled, axis=-1, keepdims=True)
        - normed * jnp.mean(scaled * normed, axis=-1, keepdims=True)
    )


def gelu_parts(pre):
    bell = 0.5 * (1.0 + jax.scipy.special.erf(pre * 0.7071067811865476))
    return pre * bell, bell + pre * jnp.exp(-0.5 * pre * pre) * 0.3989422804014327


def head_view(matrix):
    return matrix.reshape(matrix.shape[0], matrix.shape[1] // HEAD_DIM, HEAD_DIM)


def swap(value, axis, size, mask):
    return lax.ppermute(value, axis, [(i, i ^ mask) for i in range(size)])


def gather_pieces(piece, size, masks):
    held = {0: 0}
    stack = piece[None]
    for mask in masks:
        other = swap(stack, "fsdp", size, mask)
        count = stack.shape[0]
        held.update({j ^ mask: place + count for j, place in list(held.items())})
        stack = jnp.concatenate([stack, other], axis=0)
    order = [held[j] for j in sorted(held)]
    if order == list(range(len(order))):
        return stack
    return jnp.concatenate([stack[p : p + 1] for p in order], axis=0)


def gather_weights(first, second, size, axis):
    masks = [1 << k for k in range(1, size.bit_length() - 1)]
    left = gather_pieces(first, size, masks)
    right = gather_pieces(second, size, masks[::-1])
    joined = jnp.concatenate([left, right], axis=axis + 1)
    whole = jnp.concatenate([joined, swap(joined, "fsdp", size, 1)], axis=0)
    return whole.reshape(whole.shape[0] * whole.shape[1], whole.shape[2])


def add_half(kept, other):
    return (kept.astype(jnp.float32) + other.astype(jnp.float32)).astype(half_type)


def reduce_pieces(stack, size, masks):
    present = list(range(0, 2 * stack.shape[0], 2))
    for mask in masks:
        keep = [i for i, j in enumerate(present) if not j & mask]
        send = [i for i, j in enumerate(present) if j & mask]
        take = lambda which: jnp.concatenate([stack[i : i + 1] for i in which], axis=0)
        other = swap(take(send), "fsdp", size, mask)
        stack = add_half(take(keep), other)
        present = [present[i] for i in keep]
    return stack[0]


def scatter_core(gradient, size):
    half = gradient.shape[0] // 2
    other = swap(gradient[half:], "fsdp", size, 1)
    summed = add_half(gradient[:half], other)
    return summed.reshape(size // 2, 2 * half // size, gradient.shape[1])


def scatter_gradient(gradient, size, axis):
    masks = [1 << k for k in range(1, size.bit_length() - 1)]
    stack = scatter_core(gradient.astype(half_type), size)
    cut = stack.shape[axis + 1] // 2
    left = lax.slice_in_dim(stack, 0, cut, axis=axis + 1)
    right = lax.slice_in_dim(stack, cut, None, axis=axis + 1)
    return reduce_pieces(left, size, masks), reduce_pieces(right, size, masks[::-1])


def sum_everywhere(value, axis, size):
    mask = 1
    while mask < size:
        value = value + swap(value, axis, size, mask)
        mask *= 2
    return value


def placed(piece, total_width, position):
    return lax.dynamic_update_slice(
        jnp.zeros((total_width,), jnp.float32), piece, (position * piece.shape[0],)
    )


def per_device(
    fsdp,
    tp,
    layer_input,
    seq_lengths,
    query_weight,
    query_bias,
    key_weight,
    value_weight,
    value_bias,
    output_weight,
    output_bias,
    first_gain,
    first_shift,
    inner_weight,
    inner_bias,
    outer_weight,
    outer_bias,
    second_gain,
    second_shift,
    cotangent,
):
    tokens, width = layer_input.shape
    heads_width = query_weight.shape[1]
    hidden_width = inner_weight.shape[1]
    here = lax.axis_index("fsdp")
    level = lax.axis_index("tp")
    seq_length = seq_lengths[0]
    others = range(1, tp)

    rows_in = jnp.concatenate(
        [layer_input] + [swap(layer_input, "tp", tp, j) for j in others], axis=0
    )

    rows = query_weight.shape[0]
    packed = jnp.concatenate([query_weight, key_weight, value_weight], axis=1)
    attention_weights = gather_weights(packed[: rows // 2], packed[rows // 2 :], fsdp, 0)
    outer_turned = outer_weight.T
    output_turned = output_weight.T
    mlp_own = gather_weights(inner_weight, outer_turned, fsdp, 1)
    output_row = jnp.concatenate(
        [output_turned] + [swap(output_turned, "tp", tp, j) for j in others], axis=1
    )
    middle = output_row.shape[1] // 2
    output_whole = gather_weights(output_row[:, :middle], output_row[:, middle:], fsdp, 1)
    far = [mask for mask in range(2, tp, 2)]
    mlp_parts = [mlp_own]
    bias_parts = [inner_bias]
    for mask in far:
        mlp_parts.append(
            gather_weights(
                swap(inner_weight, "tp", tp, mask), swap(outer_turned, "tp", tp, mask), fsdp, 1
            )
        )
        bias_parts.append(swap(inner_bias, "tp", tp, mask))
    inner_all = jnp.concatenate([part[:, :hidden_width] for part in mlp_parts], axis=1)
    outer_all = jnp.concatenate([part[:, hidden_width:] for part in mlp_parts], axis=1)
    bias_all = jnp.concatenate(bias_parts, axis=0)

    block = width // fsdp
    place = jnp.arange(width, dtype=jnp.int32)
    piece = place // block
    apart = 2 * (piece % (fsdp // 2)) + piece // (fsdp // 2)
    feature = jnp.bitwise_xor(apart, here) * block + place % block
    shuffle = place[:, None] == feature[None, :]
    shuffle_half = shuffle.astype(half_type)
    shuffle_full = shuffle.astype(jnp.float32)

    def exact(value, turned):
        return lax.dot_general(
            value,
            shuffle_full,
            (((1,), (1 if turned else 0,)), ((), ())),
            precision=lax.Precision.HIGHEST,
            preferred_element_type=jnp.float32,
        )

    vectors = exact(
        jnp.stack([output_bias, first_gain, first_shift, outer_bias, second_gain, second_shift]),
        False,
    )
    output_bias, first_gain, first_shift, outer_bias, second_gain, second_shift = vectors
    group_rows = matmul(rows_in, shuffle_half).astype(half_type)
    own_rows = group_rows[:tokens]
    upstream = matmul(cotangent, shuffle_half)

    projected = matmul(group_rows, attention_weights)
    queries = (projected[:, :heads_width] + query_bias).astype(half_type)
    key_rows = projected[:, heads_width : 2 * heads_width].astype(half_type)
    value_rows = (projected[:, 2 * heads_width :] + value_bias).astype(half_type)
    query_heads = head_view(queries)
    key_heads = head_view(key_rows)
    value_heads = head_view(value_rows)
    slot = jnp.arange(tp * tokens, dtype=jnp.int32)
    position = jnp.bitwise_xor(slot // tokens, level) * tokens + slot % tokens
    valid = (position < seq_length)[None, None, :]

    def scores_of():
        scores = jnp.einsum(
            "qhd,khd->hqk", query_heads, key_heads, preferred_element_type=jnp.float32
        ) * HEAD_DIM ** (-0.5)
        return jnp.where(valid, scores, -jnp.inf)

    scores = scores_of()
    top = jnp.max(scores, axis=-1, keepdims=True)
    lse = top + jnp.log(jnp.sum(jnp.exp(scores - top), axis=-1, keepdims=True))
    probs = jnp.exp(scores - lse)
    context = jnp.einsum(
        "hqk,khd->qhd", probs.astype(half_type), value_heads, preferred_element_type=jnp.float32
    )
    context = context.reshape(queries.shape).astype(half_type)
    context_own = jnp.concatenate(
        [context[:tokens]]
        + [swap(context[j * tokens : (j + 1) * tokens], "tp", tp, j) for j in others],
        axis=1,
    )

    attended = right_transposed(context_own, output_whole)
    first_sum = own_rows.astype(jnp.float32) + attended + output_bias
    hidden, first_normed, first_inverse = layer_norm(first_sum, first_gain, first_shift)
    hidden_half = hidden.astype(half_type)
    hidden_rows = jnp.concatenate([hidden_half, swap(hidden_half, "tp", tp, 1)], axis=0)

    def from_pair(partial):
        mine, theirs = partial[:tokens], partial[tokens:].astype(half_type)
        return mine + swap(theirs, "tp", tp, 1).astype(jnp.float32)

    pre = matmul(hidden_rows, inner_all) + bias_all
    gelu, slope = gelu_parts(pre)
    active = gelu.astype(half_type)
    mixed = from_pair(right_transposed(active, outer_all))
    second_sum = hidden + mixed + outer_bias
    result, second_normed, second_inverse = layer_norm(second_sum, second_gain, second_shift)
    layer_output = right_transposed(result.astype(half_type), shuffle_half).astype(half_type)

    second_gain_part = jnp.sum(upstream * second_normed, axis=0)
    second_shift_part = jnp.sum(upstream, axis=0)
    grad_second = norm_backward(upstream, second_normed, second_inverse, second_gain)
    outer_bias_part = jnp.sum(grad_second, axis=0)
    second_half = grad_second.astype(half_type)
    second_rows = jnp.concatenate([second_half, swap(second_half, "tp", tp, 1)], axis=0)
    grad_pre = matmul(second_rows, outer_all) * slope
    grad_pre_half = grad_pre.astype(half_type)
    grad_hidden = grad_second + from_pair(right_transposed(grad_pre_half, inner_all))
    outer_grad = transposed(second_rows, active)
    inner_grad = transposed(hidden_rows, grad_pre_half)
    inner_bias_part = jnp.sum(grad_pre, axis=0)
    first_gain_part = jnp.sum(grad_hidden * first_normed, axis=0)
    first_shift_part = jnp.sum(grad_hidden, axis=0)
    grad_first = norm_backward(grad_hidden, first_normed, first_inverse, first_gain)
    output_bias_part = jnp.sum(grad_first, axis=0)
    first_half = grad_first.astype(half_type)
    grad_context_own = matmul(first_half, output_whole).astype(half_type)
    grad_context = jnp.concatenate(
        [grad_context_own[:, :heads_width]]
        + [
            swap(grad_context_own[:, j * heads_width : (j + 1) * heads_width], "tp", tp, j)
            for j in others
        ],
        axis=0,
    )
    output_grad = transposed(first_half, context_own)

    context_heads = head_view(grad_context)
    probs_full = jnp.exp(scores_of() - lse)
    grad_value = jnp.einsum(
        "hqk,qhd->khd", probs_full.astype(half_type), context_heads, preferred_element_type=jnp.float32
    ).reshape(queries.shape)
    grad_probs = jnp.einsum(
        "qhd,khd->hqk", context_heads, value_heads, preferred_element_type=jnp.float32
    )
    delta = jnp.sum(probs_full * grad_probs, axis=-1, keepdims=True)
    grad_scores = (probs_full * (grad_probs - delta) * HEAD_DIM ** (-0.5)).astype(half_type)
    grad_query = jnp.einsum(
        "hqk,khd->qhd", grad_scores, key_heads, preferred_element_type=jnp.float32
    ).reshape(queries.shape)
    grad_key = jnp.einsum(
        "hqk,qhd->khd", grad_scores, query_heads, preferred_element_type=jnp.float32
    ).reshape(queries.shape)
    query_bias_part = jnp.sum(grad_query, axis=0)
    value_bias_part = jnp.sum(grad_value, axis=0)
    grad_projected = jnp.concatenate([grad_query, grad_key, grad_value], axis=1).astype(half_type)
    terms = right_transposed(grad_projected, attention_weights).astype(half_type)
    attention_grad = transposed(group_rows, grad_projected)
    input_sum = grad_first + terms[:tokens].astype(jnp.float32)
    for j in others:
        input_sum = input_sum + swap(
            terms[j * tokens : (j + 1) * tokens], "tp", tp, j
        ).astype(jnp.float32)
    input_grad = exact(input_sum, True)

    def mlp_done(gradient):
        parts = []
        masks = [1 << k for k in range(1, fsdp.bit_length() - 1)]
        stack = scatter_core(gradient.astype(half_type), fsdp)
        for index in range(len(far) + 1):
            part = stack[:, :, index * hidden_width : (index + 1) * hidden_width]
            parts.append(reduce_pieces(part, fsdp, masks[::-1] if index % 2 == 0 else masks))
        total = parts[0].astype(jnp.float32)
        for mask, part in zip(far, parts[1:]):
            total = total + swap(part, "tp", tp, mask).astype(jnp.float32)
        return total

    outer_done = mlp_done(outer_grad).T
    inner_done = mlp_done(inner_grad)
    output_pieces = jnp.concatenate(scatter_gradient(output_grad, fsdp, 1), axis=1)
    output_done = output_pieces[:, :heads_width].astype(jnp.float32)
    for j in others:
        output_done = output_done + swap(
            output_pieces[:, j * heads_width : (j + 1) * heads_width], "tp", tp, j
        ).astype(jnp.float32)
    output_done = output_done.T
    attention_done = jnp.concatenate(scatter_gradient(attention_grad, fsdp, 0), axis=0).astype(
        jnp.float32
    )

    model_parts = exact(
        jnp.stack(
            [
                output_bias_part,
                first_gain_part,
                first_shift_part,
                outer_bias_part,
                second_gain_part,
                second_shift_part,
            ]
        ),
        True,
    )
    inner_total = placed(inner_bias_part[:hidden_width], tp * hidden_width, level)
    for index, mask in enumerate(far):
        inner_total = inner_total + placed(
            inner_bias_part[(index + 1) * hidden_width : (index + 2) * hidden_width],
            tp * hidden_width,
            jnp.bitwise_xor(level, mask),
        )
    early = jnp.concatenate([model_parts.reshape(-1), inner_total]).reshape(-1, 128)
    early = sum_everywhere(sum_everywhere(early, "fsdp", fsdp), "tp", tp).reshape(-1)
    late = jnp.concatenate(
        [
            placed(query_bias_part, tp * heads_width, level),
            placed(value_bias_part, tp * heads_width, level),
        ]
    ).reshape(-1, 128)
    late = sum_everywhere(sum_everywhere(late, "fsdp", fsdp), "tp", tp).reshape(-1)
    (
        output_bias_grad,
        first_gain_grad,
        first_shift_grad,
        outer_bias_grad,
        second_gain_grad,
        second_shift_grad,
    ) = [early[i * width : (i + 1) * width] for i in range(6)]
    inner_bias_grad = early[6 * width :]
    return (
        layer_output,
        input_grad,
        attention_done[:, :heads_width],
        late[: tp * heads_width],
        attention_done[:, heads_width : 2 * heads_width],
        attention_done[:, 2 * heads_width :],
        late[tp * heads_width :],
        output_done,
        output_bias_grad,
        first_gain_grad,
        first_shift_grad,
        inner_done,
        inner_bias_grad,
        outer_done,
        outer_bias_grad,
        second_gain_grad,
        second_shift_grad,
    )


def solution(mesh):
    in_specs = (
        P(("fsdp", "tp"), None),
        P("fsdp"),
        P("fsdp", "tp"),
        P("tp"),
        P("fsdp", "tp"),
        P("fsdp", "tp"),
        P("tp"),
        P("tp", "fsdp"),
        P(),
        P(),
        P(),
        P("fsdp", "tp"),
        P("tp"),
        P("tp", "fsdp"),
        P(),
        P(),
        P(),
        P(("fsdp", "tp"), None),
    )
    out_specs = (
        P(("fsdp", "tp"), None),
        P(("fsdp", "tp"), None),
        P("fsdp", "tp"),
        P(),
        P("fsdp", "tp"),
        P("fsdp", "tp"),
        P(),
        P("tp", "fsdp"),
        P(),
        P(),
        P(),
        P("fsdp", "tp"),
        P(),
        P("tp", "fsdp"),
        P(),
        P(),
        P(),
    )
    fsdp, tp = mesh.shape["fsdp"], mesh.shape["tp"]

    def body(*args):
        return per_device(fsdp, tp, *args)

    return jax.shard_map(
        body, mesh=mesh, in_specs=in_specs, out_specs=out_specs, check_vma=False
    )
```

```python
import jax
import jax.numpy as jnp
from jax import lax
from jax.sharding import PartitionSpec as P


HEAD_DIM = 64
epsilon = 1e-05
half_type = jnp.bfloat16


def matmul(left, right):
    return jnp.dot(left, right, preferred_element_type=jnp.float32)


def transposed(left, right):
    return lax.dot_general(
        left, right, (((0,), (0,)), ((), ())), preferred_element_type=jnp.float32
    )


def right_transposed(left, right):
    return lax.dot_general(
        left, right, (((1,), (1,)), ((), ())), preferred_element_type=jnp.float32
    )


def layer_norm(values, gain, shift):
    centre = values - jnp.mean(values, axis=-1, keepdims=True)
    inverse = lax.rsqrt(jnp.mean(centre * centre, axis=-1, keepdims=True) + epsilon)
    normed = centre * inverse
    return (normed * gain + shift, normed, inverse)


def norm_backward(upstream, normed, inverse, gain):
    scaled = upstream * gain
    return inverse * (
        scaled
        - jnp.mean(scaled, axis=-1, keepdims=True)
        - normed * jnp.mean(scaled * normed, axis=-1, keepdims=True)
    )


def gelu_parts(pre):
    bell = 0.5 * (1.0 + jax.scipy.special.erf(pre * 0.7071067811865476))
    return pre * bell, bell + pre * jnp.exp(-0.5 * pre * pre) * 0.3989422804014327


def head_view(matrix):
    return matrix.reshape(matrix.shape[0], matrix.shape[1] // HEAD_DIM, HEAD_DIM)


def swap(value, axis, size, mask):
    return lax.ppermute(value, axis, [(i, i ^ mask) for i in range(size)])


def routes(size):
    masks = [1 << k for k in range(1, size.bit_length() - 1)]
    return masks, masks[::-1]


def differences(masks):
    found = [0]
    for mask in masks:
        found = found + [j ^ mask for j in found]
    return found


def with_core(joined, size):
    other = swap(joined, "fsdp", size, 1)
    return jnp.concatenate([joined, other], axis=0)


def gather_two(shard, size):
    middle = shard.shape[0] // 2
    stacks = [shard[:middle], shard[middle:]]
    for k in range(len(routes(size)[0])):
        for h, masks in enumerate(routes(size)):
            other = swap(stacks[h], "fsdp", size, masks[k])
            stacks[h] = jnp.concatenate([stacks[h], other], axis=0)
    return with_core(jnp.concatenate(stacks, axis=0), size)


def gather_one(shard, size):
    rows = shard.shape[0]
    first, second = routes(size)
    stack = shard
    for mask in second:
        stack = jnp.concatenate([stack, swap(stack, "fsdp", size, mask)], axis=0)
    found = differences(second)
    parts = []
    for h, masks in enumerate((first, second)):
        for j in differences(masks):
            start = found.index(j) * rows + h * (rows // 2)
            parts.append(stack[start : start + rows // 2])
    return with_core(jnp.concatenate(parts, axis=0), size)


def add_half(kept, other):
    return (kept.astype(jnp.float32) + other.astype(jnp.float32)).astype(half_type)


def scatter_core(gradient, size):
    half = gradient.shape[0] // 2
    other = swap(gradient[half:], "fsdp", size, 1)
    return add_half(gradient[:half], other)


def scatter_two(gradient, size):
    total = scatter_core(gradient, size)
    middle = total.shape[0] // 2
    stacks = [total[:middle], total[middle:]]
    for k in reversed(range(len(routes(size)[0]))):
        for h, masks in enumerate(routes(size)):
            cut = stacks[h].shape[0] // 2
            other = swap(stacks[h][cut:], "fsdp", size, masks[k])
            stacks[h] = add_half(stacks[h][:cut], other)
    return jnp.concatenate(stacks, axis=0)


def scatter_one(gradient, size):
    total = scatter_core(gradient, size)
    rows = total.shape[0] // size
    parts = {}
    for h, masks in enumerate(routes(size)):
        for s, j in enumerate(differences(masks)):
            start = (h * (size // 2) + s) * rows
            parts[h, j] = total[start : start + rows]
    for mask in routes(size)[1]:
        keep = [key for key in parts if not key[1] & mask]
        kept = jnp.concatenate([parts[key] for key in keep], axis=0)
        sent = jnp.concatenate([parts[h, j | mask] for h, j in keep], axis=0)
        total = add_half(kept, swap(sent, "fsdp", size, mask))
        parts = {key: total[i * rows : (i + 1) * rows] for i, key in enumerate(keep)}
    return total


def sum_everywhere(value, axis, size):
    for k in range(size.bit_length() - 1):
        value = value + swap(value, axis, size, 1 << k)
    return value


def placed(piece, total_width, position):
    return lax.dynamic_update_slice(
        jnp.zeros((total_width,), jnp.float32), piece, (position * piece.shape[0],)
    )


def per_device(
    fsdp,
    tp,
    layer_input,
    seq_lengths,
    query_weight,
    query_bias,
    key_weight,
    value_weight,
    value_bias,
    output_weight,
    output_bias,
    first_gain,
    first_shift,
    inner_weight,
    inner_bias,
    outer_weight,
    outer_bias,
    second_gain,
    second_shift,
    cotangent,
):
    tokens, width = layer_input.shape
    heads_width = query_weight.shape[1]
    hidden_width = inner_weight.shape[1]
    here = lax.axis_index("fsdp")
    level = lax.axis_index("tp")
    seq_length = seq_lengths[0]
    others = range(1, tp)

    rows_in = jnp.concatenate(
        [layer_input] + [swap(layer_input, "tp", tp, j) for j in others], axis=0
    )

    packed = jnp.concatenate([query_weight, key_weight, value_weight], axis=1)
    attention_weights = gather_one(packed, fsdp)
    outer_turned = outer_weight.T
    output_row = output_weight.T
    for mask in (1, 2):
        other = swap(output_row, "tp", tp, mask)
        output_row = jnp.concatenate([output_row, other], axis=1)
    pair = jnp.concatenate([inner_weight, outer_turned], axis=1)
    own_all = gather_two(jnp.concatenate([pair, output_row], axis=1), fsdp)
    far_all = gather_two(swap(pair, "tp", tp, 2), fsdp)
    output_whole = own_all[:, 2 * hidden_width :]
    inner_all = jnp.concatenate([own_all[:, :hidden_width], far_all[:, :hidden_width]], axis=1)
    outer_all = jnp.concatenate(
        [own_all[:, hidden_width : 2 * hidden_width], far_all[:, hidden_width:]], axis=1
    )
    bias_all = jnp.concatenate([inner_bias, swap(inner_bias, "tp", tp, 2)], axis=0)

    half_block = width // fsdp // 2
    place = jnp.arange(width, dtype=jnp.int32)
    apart = jnp.asarray(
        [j + core for core in (0, 1) for masks in routes(fsdp) for j in differences(masks)],
        jnp.int32,
    )
    side = jnp.asarray([h for _ in range(2) for h in (0, 1) for _ in range(fsdp // 2)], jnp.int32)
    start = (jnp.bitwise_xor(apart, here) * 2 + side) * half_block
    feature = jnp.repeat(start, half_block) + place % half_block
    shuffle = place[:, None] == feature[None, :]
    shuffle_half = shuffle.astype(half_type)
    shuffle_full = shuffle.astype(jnp.float32)

    def exact(value, turned):
        return lax.dot_general(
            value,
            shuffle_full,
            (((1,), (1 if turned else 0,)), ((), ())),
            precision=lax.Precision.HIGHEST,
            preferred_element_type=jnp.float32,
        )

    vectors = exact(
        jnp.stack([output_bias, first_gain, first_shift, outer_bias, second_gain, second_shift]),
        False,
    )
    output_bias, first_gain, first_shift, outer_bias, second_gain, second_shift = vectors
    group_rows = matmul(rows_in, shuffle_half).astype(half_type)
    own_rows = group_rows[:tokens]
    upstream = matmul(cotangent, shuffle_half)

    projected = matmul(group_rows, attention_weights)
    queries = (projected[:, :heads_width] + query_bias).astype(half_type)
    key_rows = projected[:, heads_width : 2 * heads_width].astype(half_type)
    value_rows = (projected[:, 2 * heads_width :] + value_bias).astype(half_type)
    query_heads = head_view(queries)
    key_heads = head_view(key_rows)
    value_heads = head_view(value_rows)
    slot = jnp.arange(tp * tokens, dtype=jnp.int32)
    position = jnp.bitwise_xor(slot // tokens, level) * tokens + slot % tokens
    valid = (position < seq_length)[None, None, :]

    def scores_of():
        scores = jnp.einsum(
            "qhd,khd->hqk", query_heads, key_heads, preferred_element_type=jnp.float32
        ) * HEAD_DIM ** (-0.5)
        return jnp.where(valid, scores, -jnp.inf)

    scores = scores_of()
    top = jnp.max(scores, axis=-1, keepdims=True)
    lse = top + jnp.log(jnp.sum(jnp.exp(scores - top), axis=-1, keepdims=True))
    probs = jnp.exp(scores - lse)
    context = jnp.einsum(
        "hqk,khd->qhd", probs.astype(half_type), value_heads, preferred_element_type=jnp.float32
    )
    context = context.reshape(queries.shape).astype(half_type)
    context_own = jnp.concatenate(
        [context[:tokens]]
        + [swap(context[j * tokens : (j + 1) * tokens], "tp", tp, j) for j in others],
        axis=1,
    )

    attended = right_transposed(context_own, output_whole)
    first_sum = own_rows.astype(jnp.float32) + attended + output_bias
    hidden, first_normed, first_inverse = layer_norm(first_sum, first_gain, first_shift)
    hidden_half = hidden.astype(half_type)
    hidden_rows = jnp.concatenate([hidden_half, swap(hidden_half, "tp", tp, 1)], axis=0)

    def from_pair(partial):
        mine, theirs = partial[:tokens], partial[tokens:].astype(half_type)
        return mine + swap(theirs, "tp", tp, 1).astype(jnp.float32)

    pre = matmul(hidden_rows, inner_all) + bias_all
    gelu, slope = gelu_parts(pre)
    active = gelu.astype(half_type)
    mixed = from_pair(right_transposed(active, outer_all))
    second_sum = hidden + mixed + outer_bias
    result, second_normed, second_inverse = layer_norm(second_sum, second_gain, second_shift)
    layer_output = right_transposed(result.astype(half_type), shuffle_half).astype(half_type)

    second_gain_part = jnp.sum(upstream * second_normed, axis=0)
    second_shift_part = jnp.sum(upstream, axis=0)
    grad_second = norm_backward(upstream, second_normed, second_inverse, second_gain)
    outer_bias_part = jnp.sum(grad_second, axis=0)
    second_half = grad_second.astype(half_type)
    second_rows = jnp.concatenate([second_half, swap(second_half, "tp", tp, 1)], axis=0)
    grad_pre = matmul(second_rows, outer_all) * slope
    grad_pre_half = grad_pre.astype(half_type)
    grad_hidden = grad_second + from_pair(right_transposed(grad_pre_half, inner_all))
    outer_grad = transposed(second_rows, active)
    inner_grad = transposed(hidden_rows, grad_pre_half)
    inner_bias_part = jnp.sum(grad_pre, axis=0)
    first_gain_part = jnp.sum(grad_hidden * first_normed, axis=0)
    first_shift_part = jnp.sum(grad_hidden, axis=0)
    grad_first = norm_backward(grad_hidden, first_normed, first_inverse, first_gain)
    output_bias_part = jnp.sum(grad_first, axis=0)
    first_half = grad_first.astype(half_type)
    grad_context_own = matmul(first_half, output_whole).astype(half_type)
    grad_context = jnp.concatenate(
        [grad_context_own[:, :heads_width]]
        + [
            swap(grad_context_own[:, j * heads_width : (j + 1) * heads_width], "tp", tp, j)
            for j in others
        ],
        axis=0,
    )
    output_grad = transposed(first_half, context_own)

    context_heads = head_view(grad_context)
    probs_full = jnp.exp(scores_of() - lse)
    grad_value = jnp.einsum(
        "hqk,qhd->khd", probs_full.astype(half_type), context_heads, preferred_element_type=jnp.float32
    ).reshape(queries.shape)
    grad_probs = jnp.einsum(
        "qhd,khd->hqk", context_heads, value_heads, preferred_element_type=jnp.float32
    )
    delta = jnp.sum(probs_full * grad_probs, axis=-1, keepdims=True)
    grad_scores = (probs_full * (grad_probs - delta) * HEAD_DIM ** (-0.5)).astype(half_type)
    grad_query = jnp.einsum(
        "hqk,khd->qhd", grad_scores, key_heads, preferred_element_type=jnp.float32
    ).reshape(queries.shape)
    grad_key = jnp.einsum(
        "hqk,qhd->khd", grad_scores, query_heads, preferred_element_type=jnp.float32
    ).reshape(queries.shape)
    query_bias_part = jnp.sum(grad_query, axis=0)
    value_bias_part = jnp.sum(grad_value, axis=0)
    grad_projected = jnp.concatenate([grad_query, grad_key, grad_value], axis=1).astype(half_type)
    terms = right_transposed(grad_projected, attention_weights).astype(half_type)
    attention_grad = transposed(group_rows, grad_projected)
    input_sum = grad_first + terms[:tokens].astype(jnp.float32)
    for j in others:
        input_sum = input_sum + swap(
            terms[j * tokens : (j + 1) * tokens], "tp", tp, j
        ).astype(jnp.float32)
    input_grad = exact(input_sum, True)

    mlp_grad = jnp.concatenate(
        [
            inner_grad[:, :hidden_width],
            outer_grad[:, :hidden_width],
            inner_grad[:, hidden_width:],
            outer_grad[:, hidden_width:],
        ],
        axis=1,
    ).astype(half_type)
    mlp_pieces = scatter_two(mlp_grad, fsdp)
    mlp_far = swap(mlp_pieces[:, 2 * hidden_width :], "tp", tp, 2)
    mlp_done = mlp_pieces[:, : 2 * hidden_width].astype(jnp.float32) + mlp_far.astype(jnp.float32)
    inner_done = mlp_done[:, :hidden_width]
    outer_done = mlp_done[:, hidden_width:].T
    output_pieces = scatter_one(output_grad.astype(half_type), fsdp)
    two_heads = 2 * heads_width
    sent = jnp.concatenate(
        [output_pieces[:, heads_width:two_heads], output_pieces[:, 3 * heads_width :]], axis=1
    )
    kept = jnp.concatenate(
        [output_pieces[:, :heads_width], output_pieces[:, two_heads : 3 * heads_width]], axis=1
    )
    near = add_half(kept, swap(sent, "tp", tp, 1))
    output_done = near[:, :heads_width].astype(jnp.float32) + swap(
        near[:, heads_width:], "tp", tp, 2
    ).astype(jnp.float32)
    output_done = output_done.T
    attention_done = scatter_one(attention_grad.astype(half_type), fsdp).astype(jnp.float32)

    model_parts = exact(
        jnp.stack(
            [
                output_bias_part,
                first_gain_part,
                first_shift_part,
                outer_bias_part,
                second_gain_part,
                second_shift_part,
            ]
        ),
        True,
    )
    inner_total = placed(inner_bias_part[:hidden_width], tp * hidden_width, level) + placed(
        inner_bias_part[hidden_width:], tp * hidden_width, jnp.bitwise_xor(level, 2)
    )
    small = jnp.concatenate(
        [
            model_parts.reshape(-1),
            inner_total,
            placed(query_bias_part, tp * heads_width, level),
            placed(value_bias_part, tp * heads_width, level),
        ]
    ).reshape(-1, 128)
    small = sum_everywhere(small, "fsdp", fsdp)
    small = sum_everywhere(small, "tp", tp).reshape(-1)
    (
        output_bias_grad,
        first_gain_grad,
        first_shift_grad,
        outer_bias_grad,
        second_gain_grad,
        second_shift_grad,
    ) = [small[i * width : (i + 1) * width] for i in range(6)]
    inner_bias_grad = small[6 * width : 6 * width + tp * hidden_width]
    late = small[6 * width + tp * hidden_width :]
    return (
        layer_output,
        input_grad,
        attention_done[:, :heads_width],
        late[: tp * heads_width],
        attention_done[:, heads_width : 2 * heads_width],
        attention_done[:, 2 * heads_width :],
        late[tp * heads_width :],
        output_done,
        output_bias_grad,
        first_gain_grad,
        first_shift_grad,
        inner_done,
        inner_bias_grad,
        outer_done,
        outer_bias_grad,
        second_gain_grad,
        second_shift_grad,
    )


def solution(mesh):
    in_specs = (
        P(("fsdp", "tp"), None),
        P("fsdp"),
        P("fsdp", "tp"),
        P("tp"),
        P("fsdp", "tp"),
        P("fsdp", "tp"),
        P("tp"),
        P("tp", "fsdp"),
        P(),
        P(),
        P(),
        P("fsdp", "tp"),
        P("tp"),
        P("tp", "fsdp"),
        P(),
        P(),
        P(),
        P(("fsdp", "tp"), None),
    )
    out_specs = (
        P(("fsdp", "tp"), None),
        P(("fsdp", "tp"), None),
        P("fsdp", "tp"),
        P(),
        P("fsdp", "tp"),
        P("fsdp", "tp"),
        P(),
        P("tp", "fsdp"),
        P(),
        P(),
        P(),
        P("fsdp", "tp"),
        P(),
        P("tp", "fsdp"),
        P(),
        P(),
        P(),
    )
    fsdp, tp = mesh.shape["fsdp"], mesh.shape["tp"]

    def body(*args):
        return per_device(fsdp, tp, *args)

    return jax.shard_map(
        body, mesh=mesh, in_specs=in_specs, out_specs=out_specs, check_vma=False
    )
```

```python
import functools

import jax
import jax.numpy as jnp
from jax import lax
from jax.experimental import pallas as pl
from jax.experimental.pallas import tpu as pltpu
from jax.sharding import PartitionSpec as P


HEAD_DIM = 64
epsilon = 1e-05
LIMIT = 16 << 20
bf16 = jnp.bfloat16
f32 = jnp.float32


def matmul(left, right):
    return jnp.dot(left, right, preferred_element_type=f32)


def transposed(left, right):
    return lax.dot_general(left, right, (((0,), (0,)), ((), ())), preferred_element_type=f32)


def right_transposed(left, right):
    return lax.dot_general(left, right, (((1,), (1,)), ((), ())), preferred_element_type=f32)


def split_exact(value):
    high = value.astype(bf16)
    rest = value - high.astype(f32)
    middle = rest.astype(bf16)
    return high, middle, (rest - middle.astype(f32)).astype(bf16)


def reorder(value, shuffle, back):
    product = right_transposed if back else matmul
    high, middle, low = split_exact(value)
    return product(low, shuffle) + product(middle, shuffle) + product(high, shuffle)


def mean(value):
    return jnp.mean(value, axis=-1, keepdims=True)


def column_sum(value):
    return jnp.sum(value, axis=0, keepdims=True)


def layer_norm(values):
    centre = values - mean(values)
    inverse = lax.rsqrt(mean(centre * centre) + epsilon)
    return centre * inverse, inverse


def norm_backward(upstream, normed, inverse, gain):
    scaled = upstream * gain
    return inverse * (scaled - mean(scaled) - normed * mean(scaled * normed))


def halves(left_ref, right_ref, value):
    middle = left_ref.shape[0]
    return matmul(value[:, :middle], left_ref[...]) + matmul(value[:, middle:], right_ref[...])


def prepare_kernel(feature, v0, v1, v2, v3, v4, v5, shuffle, vectors, stage):
    width = shuffle.shape[0]
    rows = lax.broadcasted_iota(jnp.int32, (width, width), 0)
    shuffle[...] = jnp.where(rows == feature[...], 1.0, 0.0).astype(bf16)
    stage[...] = jnp.zeros_like(stage)
    for i, ref in enumerate((v0, v1, v2, v3, v4, v5)):
        stage[i : i + 1, :] = ref[...].reshape(1, width)
    vectors[...] = reorder(stage[...], shuffle[...], False)


def attend_kernel(
    info, x0, x1, x2, x3, shuffle, left, right, query_bias, value_bias,
    rows, projected, lse, c0, c1, c2, c3,
):
    tokens = x0.shape[0]
    width = query_bias.shape[0]
    heads = width // HEAD_DIM
    level, length = info[0], info[1]
    for j, ref in enumerate((x0, x1, x2, x3)):
        rows[j * tokens : (j + 1) * tokens, :] = matmul(ref[...], shuffle[...]).astype(bf16)
    values = halves(left, right, rows[...])
    projected[:, :width] = (values[:, :width] + query_bias[...].reshape(1, width)).astype(bf16)
    projected[:, width : 2 * width] = values[:, width : 2 * width].astype(bf16)
    projected[:, 2 * width :] = (values[:, 2 * width :] + value_bias[...].reshape(1, width)).astype(bf16)
    valid = valid_keys(level, length, tokens, rows.shape[0])
    lse[...] = jnp.zeros_like(lse)
    for h in range(heads):
        at = h * HEAD_DIM
        keys = projected[:, width + at : width + at + HEAD_DIM]
        vals = projected[:, 2 * width + at : 2 * width + at + HEAD_DIM]
        for j, out in enumerate((c0, c1, c2, c3)):
            span = slice(j * tokens, (j + 1) * tokens)
            scores = right_transposed(projected[span, at : at + HEAD_DIM], keys)
            scores = jnp.where(valid, scores * HEAD_DIM ** (-0.5), -jnp.inf)
            top = jnp.max(scores, axis=-1, keepdims=True)
            raised = jnp.exp(scores - top)
            total = jnp.sum(raised, axis=-1, keepdims=True)
            lse[span, h : h + 1] = top + jnp.log(total)
            probs = (raised * (1.0 / total)).astype(bf16)
            out[:, at : at + HEAD_DIM] = matmul(probs, vals).astype(bf16)


def valid_keys(level, length, tokens, count):
    slot = lax.broadcasted_iota(jnp.int32, (1, count), 1)
    valid = slot < -1
    for j in range(count // tokens):
        start = jnp.bitwise_xor(level, j) * tokens
        inside = (slot >= j * tokens) & (slot < (j + 1) * tokens)
        valid = valid | (inside & (slot - j * tokens + start < length))
    return valid


def output_kernel(c0, c1, c2, c3, left, right, rows, vectors, context, hidden, half, normed, inverse):
    tokens, part = c0.shape
    for j, ref in enumerate((c0, c1, c2, c3)):
        context[:, j * part : (j + 1) * part] = ref[...]
    attended = jnp.concatenate(
        [right_transposed(context[...], left[...]), right_transposed(context[...], right[...])],
        axis=1,
    )
    total = rows[:tokens, :].astype(f32) + attended + vectors[0:1, :]
    first, root = layer_norm(total)
    value = first * vectors[1:2, :] + vectors[2:3, :]
    hidden[...] = value
    half[...] = value.astype(bf16)
    normed[...] = first
    inverse[...] = jnp.broadcast_to(root, inverse.shape)


def forward_kernel(h, l0, r0, l1, r1, b0, b1, slope, active, out):
    units = b0.shape[0]
    middle = l0.shape[0]
    for b, (left, right, bias) in enumerate(((l0, r0, b0), (l1, r1, b1))):
        span = slice(b * units, (b + 1) * units)
        pre = (
            matmul(h[:, :middle], left[:, :units])
            + matmul(h[:, middle:], right[:, :units])
            + bias[...].reshape(1, units)
        )
        bell = 0.5 * (1.0 + lax.erf(pre * 0.7071067811865476))
        slope[:, span] = bell + pre * jnp.exp(-0.5 * pre * pre) * 0.3989422804014327
        active[:, span] = (pre * bell).astype(bf16)
    for k, (left, right) in enumerate(((l0, l1), (r0, r1))):
        value = right_transposed(active[:, :units], left[:, units:]) + right_transposed(
            active[:, units:], right[:, units:]
        )
        out[:, k * middle : (k + 1) * middle] = value.astype(out.dtype)


def middle_kernel(
    hidden, mine, other, vectors, shuffle, cotangent, output, grad, half, parts
):
    mixed = mine[...] + other[...].astype(f32)
    total = hidden[...] + mixed + vectors[3:4, :]
    second, root = layer_norm(total)
    result = (second * vectors[4:5, :] + vectors[5:6, :]).astype(bf16)
    output[...] = right_transposed(result, shuffle[...]).astype(bf16)
    upstream = matmul(cotangent[...], shuffle[...])
    back = norm_backward(upstream, second, root, vectors[4:5, :])
    grad[...] = back
    half[...] = back.astype(bf16)
    parts[...] = jnp.zeros_like(parts)
    parts[3:4, :] = column_sum(back)
    parts[4:5, :] = column_sum(upstream * second)
    parts[5:6, :] = column_sum(upstream)


def backward_kernel(s, l0, r0, l1, r1, slope, grad_pre, out, bias_part):
    units = slope.shape[1] // 2
    middle = l0.shape[0]
    for b, (left, right) in enumerate(((l0, r0), (l1, r1))):
        span = slice(b * units, (b + 1) * units)
        value = matmul(s[:, :middle], left[:, units:]) + matmul(s[:, middle:], right[:, units:])
        value = value * slope[:, span]
        bias_part[:, span] = column_sum(value)
        grad_pre[:, span] = value.astype(bf16)
    for k, (left, right) in enumerate(((l0, l1), (r0, r1))):
        value = right_transposed(grad_pre[:, :units], left[:, :units]) + right_transposed(
            grad_pre[:, units:], right[:, :units]
        )
        out[:, k * middle : (k + 1) * middle] = value.astype(out.dtype)


def weights_kernel(h0, h1, s0, s1, a0, a1, p0, p1, kept, sent, hidden, second, active, grad_pre):
    tokens, width = h0.shape
    units = a0.shape[1] // 2
    for whole, first, other in (
        (hidden, h0, h1), (second, s0, s1), (active, a0, a1), (grad_pre, p0, p1)
    ):
        whole[:tokens, :] = first[...]
        whole[tokens:, :] = other[...]
    for k, out in enumerate((kept, sent)):
        span = slice(k * (width // 2), (k + 1) * (width // 2))
        for b in range(2):
            at = 2 * b * units
            out[:, at : at + units] = transposed(
                hidden[:, span], grad_pre[:, b * units : (b + 1) * units]
            ).astype(bf16)
            out[:, at + units : at + 2 * units] = transposed(
                second[:, span], active[:, b * units : (b + 1) * units]
            ).astype(bf16)


def first_kernel(
    grad_second, mine, other, normed, inverse, vectors, left, right, parts_in, shuffle,
    grad, half, parts, d0, d1, d2, d3,
):
    upstream = grad_second[...] + mine[...] + other[...].astype(f32)
    back = norm_backward(upstream, normed[...], inverse[:, :1], vectors[1:2, :])
    grad[...] = back
    half[...] = back.astype(bf16)
    part = d0.shape[1]
    value = halves(left, right, half[...]).astype(bf16)
    for j, out in enumerate((d0, d1, d2, d3)):
        out[...] = value[:, j * part : (j + 1) * part]
    sums = jnp.concatenate(
        [column_sum(back), column_sum(upstream * normed[...]), column_sum(upstream), parts_in[3:8, :]],
        axis=0,
    )
    parts[...] = reorder(sums, shuffle[...], True)


def output_grad_kernel(half, context, kept, sent):
    middle = half.shape[1] // 2
    kept[...] = transposed(half[:, :middle], context[...]).astype(bf16)
    sent[...] = transposed(half[:, middle:], context[...]).astype(bf16)


def attend_back_kernel(
    info, d0, d1, d2, d3, projected, lse, rows, left, right,
    own, t1, t2, t3, kept, sent, bias_parts, grads, key_sum, value_sum,
):
    tokens = d0.shape[0]
    width = d0.shape[1]
    heads = width // HEAD_DIM
    level, length = info[0], info[1]
    valid = valid_keys(level, length, tokens, rows.shape[0])
    scale = HEAD_DIM ** (-0.5)
    for h in range(heads):
        at = h * HEAD_DIM
        keys = projected[:, width + at : width + at + HEAD_DIM]
        vals = projected[:, 2 * width + at : 2 * width + at + HEAD_DIM]
        for j, ref in enumerate((d0, d1, d2, d3)):
            span = slice(j * tokens, (j + 1) * tokens)
            queries = projected[span, at : at + HEAD_DIM]
            upstream = ref[:, at : at + HEAD_DIM]
            scores = jnp.where(valid, right_transposed(queries, keys) * scale, -jnp.inf)
            probs = jnp.exp(scores - lse[span, h : h + 1])
            grad_probs = right_transposed(upstream, vals)
            delta = jnp.sum(probs * grad_probs, axis=-1, keepdims=True)
            grad_scores = (probs * (grad_probs - delta) * scale).astype(bf16)
            value_part = transposed(probs.astype(bf16), upstream)
            key_part = transposed(grad_scores, queries)
            if j == 0:
                key_sum[...] = key_part
                value_sum[...] = value_part
            else:
                key_sum[...] += key_part
                value_sum[...] += value_part
            query = matmul(grad_scores, keys)
            add = column_sum(query)
            query_total = add if j == 0 else query_total + add
            grads[span, at : at + HEAD_DIM] = query.astype(bf16)
        grads[:, width + at : width + at + HEAD_DIM] = key_sum[...].astype(bf16)
        grads[:, 2 * width + at : 2 * width + at + HEAD_DIM] = value_sum[...].astype(bf16)
        bias_parts[0:1, at : at + HEAD_DIM] = query_total
        bias_parts[1:2, at : at + HEAD_DIM] = column_sum(value_sum[...])
    middle = left.shape[0]
    for j, out in enumerate((own, t1, t2, t3)):
        span = slice(j * tokens, (j + 1) * tokens)
        for k, ref in enumerate((left, right)):
            value = right_transposed(grads[span, :], ref[...]).astype(bf16)
            out[:, k * middle : (k + 1) * middle] = value
    for k, out in enumerate((kept, sent)):
        out[...] = transposed(rows[:, k * middle : (k + 1) * middle], grads[...]).astype(bf16)


def small_kernel(info, model, i0, i1, heads, out):
    level = info[0]
    out[...] = jnp.zeros_like(out)
    count, width = 6, model.shape[1]
    at = 0
    for i in range(count):
        for k in range(width // 128):
            out[at : at + 1, :] = model[i : i + 1, k * 128 : (k + 1) * 128]
            at += 1
    inner = i0[...] + i1[...]
    units = inner.shape[1] // 2
    for place in range(4):
        own, far = level == place, jnp.bitwise_xor(level, 2) == place
        value = jnp.where(own, inner[:, :units], jnp.where(far, inner[:, units:], 0.0))
        for k in range(units // 128):
            out[at : at + 1, :] = value[:, k * 128 : (k + 1) * 128]
            at += 1
    part = heads.shape[1]
    for i in range(2):
        for place in range(4):
            value = jnp.where(level == place, heads[i : i + 1, :], 0.0)
            out[at : at + 1, :] = value[:, :128]
            out[at + 1 : at + 2, : part - 128] = value[:, 128:]
            at += 2


def split_kernel(kept, other, *outs):
    groups = kept.shape[1] // outs[0].shape[1]
    count = len(outs) // groups
    rows, columns = outs[0].shape
    for i, out in enumerate(outs):
        at = (slice(i % count * rows, (i % count + 1) * rows), slice(i // count * columns, (i // count + 1) * columns))
        out[...] = (kept[at].astype(f32) + other[at].astype(f32)).astype(out.dtype)


def sum_kernel(count, *refs):
    outs = refs[count:]
    columns = outs[0].shape[1]
    for i, out in enumerate(outs):
        span = slice(i * columns, (i + 1) * columns)
        total = refs[0][:, span].astype(f32)
        for ref in refs[1:count]:
            total = total + ref[:, span].astype(f32)
        out[...] = total.astype(out.dtype)


def last_kernel(grad, own, t1, t2, shuffle, out):
    total = grad[...] + own[...].astype(f32)
    for ref in (t1, t2):
        total = total + ref[...].astype(f32)
    out[...] = reorder(total, shuffle[...], True)


def call(kernel, outs, *args, scratch=(), scalars=0, flops=0):
    spec = pl.BlockSpec(memory_space=pltpu.VMEM)
    size = sum(a.size * a.dtype.itemsize for a in args) + sum(
        o.size * o.dtype.itemsize for o in outs
    )
    return pl.pallas_call(
        kernel,
        out_shape=list(outs),
        in_specs=[pl.BlockSpec(memory_space=pltpu.SMEM)] * scalars + [spec] * (len(args) - scalars),
        out_specs=[spec] * len(outs),
        scratch_shapes=list(scratch),
        compiler_params=pltpu.CompilerParams(vmem_limit_bytes=LIMIT),
        cost_estimate=pl.CostEstimate(flops=flops, bytes_accessed=size, transcendentals=0),
    )(*args)


def array(shape, dtype):
    return jax.ShapeDtypeStruct(shape, dtype)


def swap(value, axis, size, mask):
    return lax.ppermute(value, axis, [(i, i ^ mask) for i in range(size)])


def rounds(size):
    bits = [1 << k for k in range(1, size.bit_length() - 1)]
    pairs = [bits[i : i + 2] for i in range(0, len(bits), 2)]
    return [[pair[0]] if len(pair) == 1 else [pair[0], pair[1], sum(pair)] for pair in pairs]


def gather(shard, size):
    stack = shard
    for masks in rounds(size):
        stack = jnp.concatenate(
            [stack] + [swap(stack, "fsdp", size, mask) for mask in masks],
            axis=0,
        )
    return stack, swap(stack, "fsdp", size, 1)


def cut_blocks(kept, sent, size, groups=1):
    other = swap(sent, "fsdp", size, 1)
    count = len(rounds(size)[-1]) + 1
    shape = (kept.shape[0] // count, kept.shape[1] // groups)
    blocks = call(
        split_kernel,
        ((array(shape, f32),) + (array(shape, bf16),) * (count - 1)) * groups,
        kept,
        other,
    )
    return [blocks[g * count : (g + 1) * count] for g in range(groups)]


def exchanged(blocks, size):
    for k, masks in reversed(list(enumerate(rounds(size)))):
        pieces = [blocks[0]] + [
            swap(block, "fsdp", size, mask)
            for mask, block in zip(masks, blocks[1:])
        ]
        if k > 0:
            total = sum(piece.astype(f32) for piece in pieces)
            count = len(rounds(size)[k - 1]) + 1
            cut = total.shape[0] // count
            blocks = [total[:cut]] + [
                total[i * cut : (i + 1) * cut].astype(bf16) for i in range(1, count)
            ]
    return pieces


def add_up(pieces, dtype, outs=1):
    shape = (pieces[0].shape[0], pieces[0].shape[1] // outs)
    return call(functools.partial(sum_kernel, len(pieces)), (array(shape, dtype),) * outs, *pieces)


def per_device(
    fsdp,
    tp,
    layer_input,
    seq_lengths,
    query_weight,
    query_bias,
    key_weight,
    value_weight,
    value_bias,
    output_weight,
    output_bias,
    first_gain,
    first_shift,
    inner_weight,
    inner_bias,
    outer_weight,
    outer_bias,
    second_gain,
    second_shift,
    cotangent,
):
    tokens, width = layer_input.shape
    part = query_weight.shape[1]
    units = inner_weight.shape[1]
    all_tokens = tp * tokens
    here = lax.axis_index("fsdp")
    level = lax.axis_index("tp")
    info = jnp.stack([level.astype(jnp.int32), seq_lengths[0]])
    others = (1, 2, 3)

    rows_far = swap(layer_input, "tp", tp, 2)
    rows_in = [layer_input, swap(layer_input, "tp", tp, 1), rows_far, swap(rows_far, "tp", tp, 1)]
    packed = jnp.concatenate([query_weight, key_weight, value_weight], axis=1)
    qkv_left, qkv_right = gather(packed, fsdp)
    output_row = output_weight.T
    for mask in (1, 2):
        other = swap(output_row, "tp", tp, mask)
        output_row = jnp.concatenate([output_row, other], axis=1)
    out_left, out_right = gather(output_row, fsdp)
    pair = jnp.concatenate([inner_weight, outer_weight.T], axis=1)
    own_left, own_right = gather(pair, fsdp)
    far_left, far_right = gather(swap(pair, "tp", tp, 2), fsdp)
    far_bias = swap(inner_bias, "tp", tp, 2)

    block = width // fsdp
    place = jnp.arange(width, dtype=jnp.int32)
    piece = place // block
    apart = 2 * (piece % (fsdp // 2)) + piece // (fsdp // 2)
    feature = jnp.bitwise_xor(apart, here) * block + place % block
    shuffle, vectors = call(
        prepare_kernel,
        (array((width, width), bf16), array((8, width), f32)),
        feature[None],
        output_bias,
        first_gain,
        first_shift,
        outer_bias,
        second_gain,
        second_shift,
        scratch=(pltpu.VMEM((8, width), f32),),
    )

    tile = array((tokens, width), bf16)
    wide = array((tokens, width), f32)
    heads = array((tokens, part), bf16)

    rows, projected, lse, *context = call(
        attend_kernel,
        (
            array((all_tokens, width), bf16),
            array((all_tokens, 3 * part), bf16),
            array((all_tokens, 128), f32),
        )
        + (heads,) * 4,
        info,
        *rows_in,
        shuffle,
        qkv_left,
        qkv_right,
        query_bias,
        value_bias,
        scalars=1,
        flops=2 * all_tokens * width * (width + 3 * part),
    )
    context = [context[0]] + [swap(context[j], "tp", tp, j) for j in others]

    context_own, hidden, hidden_half, first_normed, first_inverse = call(
        output_kernel,
        (tile, wide, tile, wide, array((tokens, 128), f32)),
        *context,
        out_left,
        out_right,
        rows,
        vectors,
        flops=2 * tokens * width * width,
    )
    hidden_other = swap(hidden_half, "tp", tp, 1)

    two = 2 * tokens

    weights = (own_left, own_right, far_left, far_right)

    def feed(half, result):
        return call(
            forward_kernel,
            (array((tokens, 2 * units), f32), array((tokens, 2 * units), bf16), result),
            half,
            *weights,
            inner_bias,
            far_bias,
            flops=8 * tokens * width * units,
        )

    slope_other, active_other, theirs = feed(hidden_other, tile)
    mixed = swap(theirs, "tp", tp, 1)
    slope_own, active_own, mine = feed(hidden_half, wide)
    layer_output, grad_second, second_half, parts = call(
        middle_kernel,
        (tile, wide, tile, array((8, width), f32)),
        hidden,
        mine,
        mixed,
        vectors,
        shuffle,
        cotangent,
        flops=4 * tokens * width * width,
    )

    second_other = swap(second_half, "tp", tp, 1)

    def feed_back(half, slope, result):
        return call(
            backward_kernel,
            (array((tokens, 2 * units), bf16), result, array((1, 2 * units), f32)),
            half,
            *weights,
            slope,
            flops=8 * tokens * width * units,
        )

    grad_pre_own, mine, inner_own = feed_back(second_half, slope_own, wide)
    grad_pre_other, theirs, inner_other = feed_back(second_other, slope_other, tile)
    back = swap(theirs, "tp", tp, 1)
    half_grad = array((width // 2, 4 * units), bf16)
    mlp_kept, mlp_sent = call(
        weights_kernel,
        (half_grad, half_grad),
        hidden_half,
        hidden_other,
        second_half,
        second_other,
        active_own,
        active_other,
        grad_pre_own,
        grad_pre_other,
        scratch=(pltpu.VMEM((two, width), bf16),) * 2 + (pltpu.VMEM((two, 2 * units), bf16),) * 2,
        flops=8 * two * width * units,
    )
    grad_first, first_half, model_parts, *grad_context = call(
        first_kernel,
        (wide, tile, array((8, width), f32)) + (heads,) * 4,
        grad_second,
        mine,
        back,
        first_normed,
        first_inverse,
        vectors,
        out_left,
        out_right,
        parts,
        shuffle,
        flops=2 * tokens * width * width,
    )
    grad_context = [grad_context[0]] + [swap(grad_context[j], "tp", tp, j) for j in others]
    half_output = array((width // 2, width), bf16)
    output_kept, output_sent = call(
        output_grad_kernel,
        (half_output, half_output),
        first_half,
        context_own,
        flops=2 * tokens * width * width,
    )
    half_qkv = array((width // 2, 3 * part), bf16)
    *terms, qkv_kept, qkv_sent, head_parts = call(
        attend_back_kernel,
        (tile,) * 4 + (half_qkv, half_qkv, array((2, part), f32)),
        info,
        *grad_context,
        projected,
        lse,
        rows,
        qkv_left,
        qkv_right,
        scratch=(
            pltpu.VMEM((all_tokens, 3 * part), bf16),
            pltpu.VMEM((all_tokens, HEAD_DIM), f32),
            pltpu.VMEM((all_tokens, HEAD_DIM), f32),
        ),
        scalars=1,
        flops=4 * all_tokens * width * 3 * part,
    )
    joined = terms[2].astype(f32) + swap(terms[3], "tp", tp, 1).astype(f32)
    (input_grad,) = call(
        last_kernel,
        (wide,),
        grad_first,
        terms[0],
        swap(terms[1], "tp", tp, 1),
        swap(joined.astype(bf16), "tp", tp, 2),
        shuffle,
        flops=6 * tokens * width * width,
    )

    blocks_own, blocks_far = cut_blocks(mlp_kept, mlp_sent, fsdp, 2)
    (mlp_far,) = add_up(exchanged(blocks_far, fsdp), bf16)
    mlp_far = swap(mlp_far, "tp", tp, 2)
    inner_done, outer_done = add_up(exchanged(blocks_own, fsdp) + [mlp_far], f32, 2)
    outer_done = outer_done.T
    (blocks,) = cut_blocks(output_kept, output_sent, fsdp)
    pieces = add_up(exchanged(blocks, fsdp), f32, tp)
    sent = jnp.concatenate([pieces[1], pieces[3]], axis=1).astype(bf16)
    other = swap(sent, "tp", tp, 1)
    last = swap((pieces[2] + other[:, part:].astype(f32)).astype(bf16), "tp", tp, 2)
    output_done = (pieces[0] + other[:, :part].astype(f32) + last.astype(f32)).T
    (blocks,) = cut_blocks(qkv_kept, qkv_sent, fsdp)
    query_done, key_done, value_done = add_up(exchanged(blocks, fsdp), f32, 3)

    lines = 6 * width + tp * units + 2 * tp * 256
    (small,) = call(
        small_kernel,
        (array((lines // 128, 128), f32),),
        info,
        model_parts,
        inner_own,
        inner_other,
        head_parts,
        scalars=1,
    )
    small = small + swap(small, "fsdp", fsdp, 1)
    for k in range(tp.bit_length() - 1):
        small = small + swap(small, "tp", tp, 1 << k)
    for k in range(1, fsdp.bit_length() - 1):
        small = small + swap(small, "fsdp", fsdp, 1 << k)
    small = small.reshape(-1)
    (
        output_bias_grad,
        first_gain_grad,
        first_shift_grad,
        outer_bias_grad,
        second_gain_grad,
        second_shift_grad,
    ) = [small[i * width : (i + 1) * width] for i in range(6)]
    late = 6 * width + tp * units
    query_bias_grad, value_bias_grad = [
        small[late + i * tp * 256 : late + (i + 1) * tp * 256]
        .reshape(tp, 256)[:, :part]
        .reshape(-1)
        for i in (0, 1)
    ]
    return (
        layer_output,
        input_grad,
        query_done,
        query_bias_grad,
        key_done,
        value_done,
        value_bias_grad,
        output_done,
        output_bias_grad,
        first_gain_grad,
        first_shift_grad,
        inner_done,
        small[6 * width : late],
        outer_done,
        outer_bias_grad,
        second_gain_grad,
        second_shift_grad,
    )


def solution(mesh):
    in_specs = (
        P(("fsdp", "tp"), None),
        P("fsdp"),
        P("fsdp", "tp"),
        P("tp"),
        P("fsdp", "tp"),
        P("fsdp", "tp"),
        P("tp"),
        P("tp", "fsdp"),
        P(),
        P(),
        P(),
        P("fsdp", "tp"),
        P("tp"),
        P("tp", "fsdp"),
        P(),
        P(),
        P(),
        P(("fsdp", "tp"), None),
    )
    out_specs = (
        P(("fsdp", "tp"), None),
        P(("fsdp", "tp"), None),
        P("fsdp", "tp"),
        P(),
        P("fsdp", "tp"),
        P("fsdp", "tp"),
        P(),
        P("tp", "fsdp"),
        P(),
        P(),
        P(),
        P("fsdp", "tp"),
        P(),
        P("tp", "fsdp"),
        P(),
        P(),
        P(),
    )
    fsdp, tp = mesh.shape["fsdp"], mesh.shape["tp"]

    def body(*args):
        return per_device(fsdp, tp, *args)

    return jax.shard_map(
        body, mesh=mesh, in_specs=in_specs, out_specs=out_specs, check_vma=False
    )
```
